32 devices in a mesh: gz: 4 (over y, x), gy: 2 (over core), gx: 4 (over z).
Axes of the slice: x: 2, y: 2, z: 4, core: 2. Of those that a mesh axis runs over, the one named last changes fastest.
Arguments:
- vectors: bfloat16 [4, 2, 4, 4, 24, 2, 4, 3, 256], P('gz', 'gy', 'gx'), may hold values from -6 to 6
- links: bfloat16 [4, 2, 4, 4, 4, 2, 3, 3, 256], P('gz', 'gy', 'gx'), may hold values from -2.5 to 2.5
- site_term: bfloat16 [4, 2, 4, 4, 2, 2, 6, 6, 256], P('gz', 'gy', 'gx'), may hold values from -3 to 3, as said below
- owner: int32 [4, 2, 4, 4], replicated, may hold values from 0 to 15, as said below
- coarse_rhs: bfloat16 [4, 2, 4, 4, 2, 24], P('gz', 'gy', 'gx'), may hold values from -50 to 50
Outputs:
- coarse_operator: bfloat16 [16, 32, 9, 2, 576], P(('gz', 'gx'))
- coarse_solution: float32 [16, 32, 2, 24], P(('gz', 'gx'))
The draws below stay inside these ranges and needn't reach their ends.
Inputs may be any that keep to these rules, and one draw needn't show every extreme that they name: Within each block of 4 aggregates with the same z, y, x no owner appears more than 1 times, and one owner appears exactly 1 times in every block. `site_term`: each chirality block is Hermitian.
All inputs are finite; a program needn't handle non-finite values.
Results may differ from the reference program's by a relative error of at most 0.009.
Values may be sent and summed in bfloat16 or wider, within the bound.
A program may use at most 128 MiB of HBM per device.

```python
import math
import jax
import jax.numpy as jnp
import numpy as np
from jax import lax

NV = 24
AT = 4
ITERS = 4
PAIR = 1
CAP = 32
N_GZ = 4
N_GY = 2
N_GX = 4


def draw_site_term(key, part):
    shape_all = (N_GZ, N_GY, N_GX, AT, 2, 2, 6, 6, 256)
    raw_draw = jnp.clip(jax.random.normal(key, shape_all, jnp.float32) * 0.5, -3.0, 3.0)
    real_part = raw_draw[:, :, :, :, :, 0]
    imag_part = raw_draw[:, :, :, :, :, 1]
    herm_re = (real_part + jnp.swapaxes(real_part, -3, -2)) * 0.5
    herm_im = (imag_part - jnp.swapaxes(imag_part, -3, -2)) * 0.5
    return jnp.stack([herm_re, herm_im], axis=5).astype(jnp.bfloat16)


def draw_coarse_rhs(key, part):
    key_base = jax.random.fold_in(key, 11)
    key_scale = jax.random.fold_in(key, 12)
    shape_all = (N_GZ, N_GY, N_GX, AT, 2, NV)
    base_draw = jnp.clip(jax.random.normal(key_base, shape_all, jnp.float32), -5.0, 5.0)
    row_scale = jnp.exp(jax.random.uniform(key_scale, (N_GZ, N_GY, N_GX, AT, 1, 1), jnp.float32, 0.0, math.log(10.0)))
    return (base_draw * row_scale).astype(jnp.bfloat16)


def draw_owner(key, part):
    block_count = N_GZ * N_GY * N_GX
    owners_count = N_GZ * N_GX
    label_count = (owners_count - 1) * PAIR
    key_full = jax.random.fold_in(key, 21)
    key_pick = jax.random.fold_in(key, 22)
    key_order = jax.random.fold_in(key, 23)
    full_owner = jax.random.randint(key_full, (), 0, owners_count, dtype=jnp.int32)
    labels = jnp.arange(label_count, dtype=jnp.int32) // PAIR
    others = labels + (labels >= full_owner).astype(jnp.int32)
    scores = jax.random.randint(key_pick, (block_count, label_count), 0, 1048576, dtype=jnp.int32) * label_count + jnp.arange(label_count, dtype=jnp.int32)
    order = jnp.argsort(scores, axis=1)
    picked = others[order[:, :AT - PAIR]]
    filled = jnp.concatenate([jnp.full((block_count, PAIR), full_owner, jnp.int32), picked], axis=1)
    scores_two = jax.random.randint(key_order, (block_count, AT), 0, 1048576, dtype=jnp.int32) * AT + jnp.arange(AT, dtype=jnp.int32)
    positions = jnp.argsort(scores_two, axis=1)
    mixed = jnp.take_along_axis(filled, positions, axis=1)
    return mixed.reshape(N_GZ, N_GY, N_GX, AT).astype(jnp.int32)


def levels(own_key, shape, cuts, low, top_value):
    level, own = 1.0, jax.random.fold_in(own_key, 6)
    for dim, parts in cuts:
        steps = jnp.exp(jax.random.uniform(jax.random.fold_in(own, dim), (parts,), jnp.float32, low / len(cuts), top_value / len(cuts)))
        level = level * jnp.repeat(steps, shape[dim] // parts).reshape([-1 if axis == dim else 1 for axis in range(len(shape))])
    return level


def bell_draw(rng, shape, deviation, limit, cuts=(), kind=jnp.bfloat16):
    entries = jax.random.normal(rng, shape, jnp.float32) * deviation
    if len(cuts) > 0:
        entries = levels(rng, shape, cuts, -0.22, 0.18) * entries
    return jnp.clip(entries, min=-limit, max=limit).astype(kind)


def setup_inputs(seed: int = 0) -> dict:
    arg_keys = jax.random.split(jax.random.key(seed), 6)
    vectors = bell_draw(arg_keys[0], (N_GZ, N_GY, N_GX, AT, NV, 2, 4, 3, 256), 1.0, 6.0, ((0, 4), (1, 2), (2, 4)))
    links = bell_draw(arg_keys[1], (N_GZ, N_GY, N_GX, AT, 4, 2, 3, 3, 256), 6 ** -0.5, 2.5, ((0, 4), (1, 2), (2, 4)))
    site_term = draw_site_term(jax.random.fold_in(arg_keys[5], 71), 0)
    owner = draw_owner(jax.random.fold_in(arg_keys[5], 71), 0)
    coarse_rhs = draw_coarse_rhs(jax.random.fold_in(arg_keys[5], 71), 0)
    return dict(vectors=vectors, links=links, site_term=site_term, owner=owner, coarse_rhs=coarse_rhs)


coarse_scale = 1.0 / 256.0
epsilon = 1e-06
site_strides = (64, 16, 4, 1)
roll_axes = (2, 1, 0, 3)

def face_table(stride, layer_index):
    position = np.arange(64)
    return position // stride * 4 * stride + position % stride + layer_index * stride

def take_sites(array_in, stride, layer_index):
    picks = jnp.asarray(face_table(stride, layer_index), dtype=jnp.int32)
    return jnp.take(array_in, picks, axis=-1)

def times_spin(direction, lower_part):
    real_zero = lower_part[..., 0, 0, :, :]
    real_one = lower_part[..., 0, 1, :, :]
    imag_zero = lower_part[..., 1, 0, :, :]
    imag_one = lower_part[..., 1, 1, :, :]
    if direction == 0:
        pieces = ((imag_one, imag_zero), (-real_one, -real_zero))
    elif direction == 1:
        pieces = ((-real_one, real_zero), (-imag_one, imag_zero))
    elif direction == 2:
        pieces = ((imag_zero, -imag_one), (-real_zero, real_one))
    else:
        return lower_part
    return jnp.stack([jnp.stack(pieces[0], -3), jnp.stack(pieces[1], -3)], -4)

def project(vectors, direction):
    spinor = vectors.astype(jnp.float32)
    upper_part = spinor[:, :, :, 0:2]
    lower_part = times_spin(direction, spinor[:, :, :, 2:4])
    return ((upper_part - lower_part).astype(jnp.bfloat16), (upper_part + lower_part).astype(jnp.bfloat16))

def transport(link_field, half_field, adjoint):
    link_field = link_field.astype(jnp.float32)
    half_field = half_field.astype(jnp.float32)
    link_re = link_field[:, 0][:, None, None]
    link_im = link_field[:, 1][:, None, None]
    half_re = half_field[:, :, 0]
    half_im = half_field[:, :, 1]
    if adjoint:
        half_re = half_re[..., :, None, :]
        half_im = half_im[..., :, None, :]
        out_re = lax.optimization_barrier(jnp.sum(link_re * half_re + link_im * half_im, axis=-3))
        out_im = lax.optimization_barrier(jnp.sum(link_re * half_im - link_im * half_re, axis=-3))
    else:
        half_re = half_re[..., None, :, :]
        half_im = half_im[..., None, :, :]
        out_re = lax.optimization_barrier(jnp.sum(link_re * half_re - link_im * half_im, axis=-2))
        out_im = lax.optimization_barrier(jnp.sum(link_re * half_im + link_im * half_re, axis=-2))
    return jnp.stack([out_re, out_im], axis=2).astype(jnp.bfloat16)

def apply_site(site_term, vectors):
    shape_in = vectors.shape
    spinor = vectors.astype(jnp.float32).reshape(shape_in[0], shape_in[1], 2, 2, 1, 6, shape_in[-1])
    matrix = site_term.astype(jnp.float32)[:, None]
    spin_re = spinor[:, :, 0]
    spin_im = spinor[:, :, 1]
    mat_re = matrix[:, :, :, 0]
    mat_im = matrix[:, :, :, 1]
    out_re = lax.optimization_barrier(jnp.sum(mat_re * spin_re - mat_im * spin_im, axis=-2))
    out_im = lax.optimization_barrier(jnp.sum(mat_re * spin_im + mat_im * spin_re, axis=-2))
    return jnp.stack([out_re, out_im], axis=2).reshape(shape_in).astype(jnp.bfloat16)

def contract(left, right):
    shape_two = (left.shape[0], left.shape[1], -1)
    left_re = left[:, :, 0].reshape(shape_two)
    left_im = left[:, :, 1].reshape(shape_two)
    right_re = right[:, :, 0].reshape(shape_two)
    right_im = right[:, :, 1].reshape(shape_two)
    first = jnp.concatenate([left_re, left_im], axis=-1).astype(jnp.float32)
    second = jnp.concatenate([right_re, right_im], axis=-1).astype(jnp.float32)
    third = jnp.concatenate([left_re, -left_im], axis=-1).astype(jnp.float32)
    fourth = jnp.concatenate([right_im, right_re], axis=-1).astype(jnp.float32)
    return (jnp.einsum('bik,bjk->bij', first, second), jnp.einsum('bik,bjk->bij', third, fourth))

def make_halves(vectors, links):
    result = []
    for direction in range(4):
        minus_half, plus_half = project(vectors, direction)
        back_half = transport(links[:, direction], plus_half, True)
        result.append((minus_half, plus_half, back_half))
    return result

def restrict(vectors, links, site_term, halves, incoming, select_sites):
    positions = jnp.arange(vectors.shape[-1], dtype=jnp.int32)
    self_re, self_im = contract(vectors, apply_site(site_term, vectors))
    blocks_out = []
    for direction in range(4):
        stride = site_strides[direction]
        coordinate = positions // stride % 4
        minus_half, plus_half, back_half = halves[direction]
        link_field = links[:, direction]
        keep_up = (coordinate < 3).astype(minus_half.dtype)
        keep_down = (coordinate > 0).astype(minus_half.dtype)
        ahead_field = transport(link_field, jnp.roll(minus_half, -stride, axis=-1) * keep_up, False)
        fwd_re, fwd_im = contract(minus_half, ahead_field)
        behind_field = jnp.roll(back_half, stride, axis=-1) * keep_down
        bwd_re, bwd_im = contract(plus_half, behind_field)
        self_re = self_re - 0.5 * (fwd_re + bwd_re)
        self_im = self_im - 0.5 * (fwd_im + bwd_im)
        from_above, from_below = incoming[direction]
        face_ahead = transport(select_sites(link_field, stride, 3), from_above, False)
        up_re, up_im = contract(select_sites(minus_half, stride, 3), face_ahead)
        down_re, down_im = contract(select_sites(plus_half, stride, 0), from_below)
        blocks_out.append(jnp.stack([up_re, up_im], 1) * (-0.5 * coarse_scale))
        blocks_out.append(jnp.stack([down_re, down_im], 1) * (-0.5 * coarse_scale))
    first_block = jnp.stack([self_re, self_im], 1) * coarse_scale
    return jnp.stack([first_block] + blocks_out, axis=1)

def complex_apply(coarse_f, stacked):
    mat_re = coarse_f[..., 0, :, :]
    mat_im = coarse_f[..., 1, :, :]
    vec_re = stacked[..., 0, :]
    vec_im = stacked[..., 1, :]
    highest = lax.Precision.HIGHEST
    out_re = jnp.einsum('...kij,...kj->...i', mat_re, vec_re, precision=highest) - jnp.einsum('...kij,...kj->...i', mat_im, vec_im, precision=highest)
    out_im = jnp.einsum('...kij,...kj->...i', mat_re, vec_im, precision=highest) + jnp.einsum('...kij,...kj->...i', mat_im, vec_re, precision=highest)
    return jnp.stack([out_re, out_im], axis=-2)

def inner_product(left, right):
    real_part = jnp.sum(left[..., 0, :] * right[..., 0, :] + left[..., 1, :] * right[..., 1, :])
    imag_part = jnp.sum(left[..., 0, :] * right[..., 1, :] - left[..., 1, :] * right[..., 0, :])
    return (real_part, imag_part)

def subtract_scaled(vector, coef, basis):
    new_re = vector[..., 0, :] - (coef[0] * basis[..., 0, :] - coef[1] * basis[..., 1, :])
    new_im = vector[..., 1, :] - (coef[0] * basis[..., 1, :] + coef[1] * basis[..., 0, :])
    return jnp.stack([new_re, new_im], axis=-2)

def complex_mul(first, second):
    return (first[0] * second[0] - first[1] * second[1], first[0] * second[1] + first[1] * second[0])

def rotate(top_entry, bottom_entry, scale_norm, upper_value, lower_value):
    conj_top = (top_entry[0], -top_entry[1])
    conj_bottom = (bottom_entry[0], -bottom_entry[1])
    part_one = complex_mul(conj_top, upper_value)
    part_two = complex_mul(conj_bottom, lower_value)
    part_three = complex_mul(bottom_entry, upper_value)
    part_four = complex_mul(top_entry, lower_value)
    new_upper = ((part_one[0] + part_two[0]) / scale_norm, (part_one[1] + part_two[1]) / scale_norm)
    new_lower = ((part_four[0] - part_three[0]) / scale_norm, (part_four[1] - part_three[1]) / scale_norm)
    return (new_upper, new_lower)

def least_squares(hessen, beta):
    columns = len(hessen[0])
    zero_value = jnp.zeros((), jnp.float32)
    matrix = [list(row_list) for row_list in hessen]
    target = [(beta, zero_value)] + [(zero_value, zero_value)] * columns
    rotations = []
    for col_index in range(columns):
        for rot_index in range(col_index):
            top_entry, bottom_entry, scale_norm = rotations[rot_index]
            pair = rotate(top_entry, bottom_entry, scale_norm, matrix[rot_index][col_index], matrix[rot_index + 1][col_index])
            matrix[rot_index][col_index] = pair[0]
            matrix[rot_index + 1][col_index] = pair[1]
        top_entry = matrix[col_index][col_index]
        bottom_entry = matrix[col_index + 1][col_index]
        scale_norm = jnp.sqrt(top_entry[0] * top_entry[0] + top_entry[1] * top_entry[1] + bottom_entry[0] * bottom_entry[0] + bottom_entry[1] * bottom_entry[1])
        rotations.append((top_entry, bottom_entry, scale_norm))
        matrix[col_index][col_index] = (scale_norm, zero_value)
        matrix[col_index + 1][col_index] = (zero_value, zero_value)
        pair = rotate(top_entry, bottom_entry, scale_norm, target[col_index], target[col_index + 1])
        target[col_index] = pair[0]
        target[col_index + 1] = pair[1]
    weights = [None] * columns
    for row_index in reversed(range(columns)):
        remainder = target[row_index]
        for col_index in range(row_index + 1, columns):
            product_term = complex_mul(matrix[row_index][col_index], weights[col_index])
            remainder = (remainder[0] - product_term[0], remainder[1] - product_term[1])
        weights[row_index] = (remainder[0] / matrix[row_index][row_index][0], remainder[1] / matrix[row_index][row_index][0])
    return weights

def rank_table(owner, owners_count):
    one_hot = (owner[..., None] == jnp.arange(owners_count, dtype=jnp.int32)).astype(jnp.int32)
    return lax.optimization_barrier(jnp.sum(jnp.cumsum(one_hot, axis=3) * one_hot, axis=-1)) - 1

def coarse_matvec(coarse_f, vector):
    neighbors = [vector]
    for axis_index in roll_axes:
        neighbors.append(jnp.roll(vector, -1, axis=axis_index))
        neighbors.append(jnp.roll(vector, 1, axis=axis_index))
    return complex_apply(coarse_f, jnp.stack(neighbors, axis=4))

def reference(vectors, links, site_term, owner, coarse_rhs):
    group_size = N_GX * AT
    block_count = N_GZ * N_GY
    flat_vec = vectors.reshape((block_count, group_size) + vectors.shape[4:])
    flat_link = links.reshape((block_count, group_size) + links.shape[4:])
    flat_site = site_term.reshape((block_count, group_size) + site_term.shape[4:])

    def send_faces(inputs):
        halves = make_halves(inputs[0], inputs[1])
        above_faces = []
        below_faces = []
        for direction in range(4):
            above_faces.append(take_sites(halves[direction][0], site_strides[direction], 0))
            below_faces.append(take_sites(halves[direction][2], site_strides[direction], 3))
        return tuple(above_faces) + tuple(below_faces)
    faces = lax.map(send_faces, (flat_vec, flat_link))
    moved = []
    for direction in range(4):
        grid_face = faces[direction].reshape((N_GZ, N_GY, N_GX, AT) + faces[direction].shape[2:])
        moved.append(jnp.roll(grid_face, -1, axis=roll_axes[direction]).reshape(faces[direction].shape))
    for direction in range(4):
        grid_face = faces[4 + direction].reshape((N_GZ, N_GY, N_GX, AT) + faces[4 + direction].shape[2:])
        moved.append(jnp.roll(grid_face, 1, axis=roll_axes[direction]).reshape(faces[4 + direction].shape))

    def coarse_block(inputs):
        halves = make_halves(inputs[0], inputs[1])
        incoming = []
        for direction in range(4):
            incoming.append((inputs[3 + direction], inputs[7 + direction]))
        return restrict(inputs[0], inputs[1], inputs[2], halves, incoming, take_sites)
    blocks = lax.map(coarse_block, (flat_vec, flat_link, flat_site) + tuple(moved))
    coarse_rows = blocks.reshape((N_GZ, N_GY, N_GX, AT, 9, 2, NV, NV)).astype(jnp.bfloat16)
    coarse_f = coarse_rows.astype(jnp.float32)
    right_side = coarse_rhs.astype(jnp.float32)
    zero_value = jnp.zeros((), jnp.float32)
    beta = jnp.sqrt(jnp.sum(right_side * right_side) + epsilon)
    basis = [right_side / beta]
    hessen = []
    for row_index in range(ITERS + 1):
        hessen.append([(zero_value, zero_value)] * ITERS)
    for column in range(ITERS):
        work = coarse_matvec(coarse_f, basis[column])
        for row_index in range(column + 1):
            coef = inner_product(basis[row_index], work)
            hessen[row_index][column] = coef
            work = subtract_scaled(work, coef, basis[row_index])
        norm_now = jnp.sqrt(jnp.sum(work * work) + epsilon)
        hessen[column + 1][column] = (norm_now, zero_value)
        basis.append(work / norm_now)
    weights = least_squares(hessen, beta)
    solution = jnp.zeros_like(right_side)
    for column in range(ITERS):
        solution = subtract_scaled(solution, (-weights[column][0], -weights[column][1]), basis[column])
    owners_count = N_GZ * N_GX
    owner_rank = rank_table(owner, owners_count)
    coord_z = lax.broadcasted_iota(jnp.int32, owner.shape, 0)
    coord_y = lax.broadcasted_iota(jnp.int32, owner.shape, 1)
    coord_x = lax.broadcasted_iota(jnp.int32, owner.shape, 2)
    location = (owner * CAP + ((coord_z * N_GX + coord_x) * N_GY + coord_y) * PAIR + owner_rank).reshape(-1).astype(jnp.int32)
    rows_out = jnp.zeros((owners_count * CAP, 9, 2, NV * NV), jnp.bfloat16)
    rows_out = rows_out.at[location].set(coarse_rows.reshape(-1, 9, 2, NV * NV))
    solution_out = jnp.zeros((owners_count * CAP, 2, NV), jnp.float32)
    solution_out = solution_out.at[location].set(solution.reshape(-1, 2, NV))
    return (rows_out.reshape(owners_count, CAP, 9, 2, NV * NV), solution_out.reshape(owners_count, CAP, 2, NV))
```

```python
import jax
import jax.numpy as jnp
import numpy as np
from jax import lax
from jax.experimental import pallas as pl
from jax.experimental.pallas import tpu as pltpu
from jax.sharding import PartitionSpec as P

NV = 24
AT = 4
ITERS = 4
PAIR = 1
LANES = 128
SLAB = 2 * NV * NV


coarse_scale = 1.0 / 256.0
epsilon = 1e-06
site_strides = (64, 16, 4, 1)
neighbor_offsets = (
    (0, 0, 0, 0),
    (0, 0, 1, 0),
    (0, 0, -1, 0),
    (0, 1, 0, 0),
    (0, -1, 0, 0),
    (1, 0, 0, 0),
    (-1, 0, 0, 0),
    (0, 0, 0, 1),
    (0, 0, 0, -1),
)


def from_behind(block, axis, distance):
    devices = range(lax.axis_size(axis))
    route = [((i - distance) % len(devices), i) for i in devices]
    return lax.ppermute(block, axis, route)


def select_sites(array_in, stride, layer_index):
    site_count = array_in.shape[-1]
    row_pos = lax.broadcasted_iota(jnp.int32, (site_count, 64), 0)
    col_pos = lax.broadcasted_iota(jnp.int32, (site_count, 64), 1)
    target = col_pos // stride * 4 * stride + col_pos % stride + layer_index * stride
    picker = (row_pos == target).astype(jnp.bfloat16)
    return jnp.einsum("...r,rf->...f", array_in, picker, preferred_element_type=jnp.float32).astype(
        jnp.bfloat16
    )


def times_spin(direction, lower_part):
    real_zero = lower_part[..., 0, 0, :, :]
    real_one = lower_part[..., 0, 1, :, :]
    imag_zero = lower_part[..., 1, 0, :, :]
    imag_one = lower_part[..., 1, 1, :, :]
    if direction == 0:
        pieces = ((imag_one, imag_zero), (-real_one, -real_zero))
    elif direction == 1:
        pieces = ((-real_one, real_zero), (-imag_one, imag_zero))
    elif direction == 2:
        pieces = ((imag_zero, -imag_one), (-real_zero, real_one))
    else:
        return lower_part
    return jnp.stack([jnp.stack(pieces[0], -3), jnp.stack(pieces[1], -3)], -4)


def project(vectors, direction):
    spinor = vectors.astype(jnp.float32)
    upper_part = spinor[:, :, :, 0:2]
    lower_part = times_spin(direction, spinor[:, :, :, 2:4])
    return (
        (upper_part - lower_part).astype(jnp.bfloat16),
        (upper_part + lower_part).astype(jnp.bfloat16),
    )


def transport(link_field, half_field, adjoint):
    link_field = link_field.astype(jnp.float32)
    half_field = half_field.astype(jnp.float32)
    link_re = link_field[:, 0][:, None, None]
    link_im = link_field[:, 1][:, None, None]
    half_re = half_field[:, :, 0]
    half_im = half_field[:, :, 1]
    if adjoint:
        half_re = half_re[..., :, None, :]
        half_im = half_im[..., :, None, :]
        out_re = jnp.sum(link_re * half_re + link_im * half_im, axis=-3)
        out_im = jnp.sum(link_re * half_im - link_im * half_re, axis=-3)
    else:
        half_re = half_re[..., None, :, :]
        half_im = half_im[..., None, :, :]
        out_re = jnp.sum(link_re * half_re - link_im * half_im, axis=-2)
        out_im = jnp.sum(link_re * half_im + link_im * half_re, axis=-2)
    return jnp.stack([out_re, out_im], axis=2).astype(jnp.bfloat16)


def apply_site(site_term, vectors):
    shape_in = vectors.shape
    spinor = vectors.astype(jnp.float32).reshape(shape_in[0], shape_in[1], 2, 2, 1, 6, shape_in[-1])
    matrix = site_term.astype(jnp.float32)[:, None]
    spin_re = spinor[:, :, 0]
    spin_im = spinor[:, :, 1]
    mat_re = matrix[:, :, :, 0]
    mat_im = matrix[:, :, :, 1]
    out_re = jnp.sum(mat_re * spin_re - mat_im * spin_im, axis=-2)
    out_im = jnp.sum(mat_re * spin_im + mat_im * spin_re, axis=-2)
    return jnp.stack([out_re, out_im], axis=2).reshape(shape_in).astype(jnp.bfloat16)


def contract(left, right):
    shape_two = (left.shape[0], left.shape[1], -1)
    left_re = left[:, :, 0].reshape(shape_two)
    left_im = left[:, :, 1].reshape(shape_two)
    right_re = right[:, :, 0].reshape(shape_two)
    right_im = right[:, :, 1].reshape(shape_two)
    first = jnp.concatenate([left_re, left_im], axis=-1)
    second = jnp.concatenate([right_re, right_im], axis=-1)
    third = jnp.concatenate([left_re, -left_im], axis=-1)
    fourth = jnp.concatenate([right_im, right_re], axis=-1)
    real_part = jnp.einsum("bik,bjk->bij", first, second, preferred_element_type=jnp.float32)
    imag_part = jnp.einsum("bik,bjk->bij", third, fourth, preferred_element_type=jnp.float32)
    return (real_part, imag_part)


def make_halves(vectors, links):
    result = []
    for direction in range(4):
        minus_half, plus_half = project(vectors, direction)
        back_half = transport(links[:, direction], plus_half, True)
        result.append((minus_half, plus_half, back_half))
    return result


def restrict(vectors, links, site_term, halves, incoming):
    positions = jnp.arange(vectors.shape[-1], dtype=jnp.int32)
    self_re, self_im = contract(vectors, apply_site(site_term, vectors))
    blocks_out = []
    for direction in range(4):
        stride = site_strides[direction]
        coordinate = positions // stride % 4
        minus_half, plus_half, back_half = halves[direction]
        link_field = links[:, direction]
        keep_up = (coordinate < 3).astype(minus_half.dtype)
        keep_down = (coordinate > 0).astype(minus_half.dtype)
        ahead_field = transport(link_field, jnp.roll(minus_half, -stride, axis=-1) * keep_up, False)
        fwd_re, fwd_im = contract(minus_half, ahead_field)
        behind_field = jnp.roll(back_half, stride, axis=-1) * keep_down
        bwd_re, bwd_im = contract(plus_half, behind_field)
        self_re = self_re - 0.5 * (fwd_re + bwd_re)
        self_im = self_im - 0.5 * (fwd_im + bwd_im)
        from_above, from_below = incoming[direction]
        face_ahead = transport(select_sites(link_field, stride, 3), from_above, False)
        up_re, up_im = contract(select_sites(minus_half, stride, 3), face_ahead)
        down_re, down_im = contract(select_sites(plus_half, stride, 0), from_below)
        blocks_out.append(jnp.stack([up_re, up_im], 1) * (-0.5 * coarse_scale))
        blocks_out.append(jnp.stack([down_re, down_im], 1) * (-0.5 * coarse_scale))
    first_block = jnp.stack([self_re, self_im], 1) * coarse_scale
    return jnp.stack([first_block] + blocks_out, axis=1)


def spinor_faces(vectors, links, direction, send_up, send_down):
    stride = site_strides[direction]
    arrived_up = send_up(select_sites(vectors, stride, 0))
    from_above, unused = project(arrived_up, direction)
    lower_face = select_sites(vectors, stride, 3)
    link_face = select_sites(links[:, direction], stride, 3)
    packed = jnp.concatenate(
        [
            lower_face.reshape(lower_face.shape[0], -1, 64),
            link_face.reshape(link_face.shape[0], -1, 64),
        ],
        axis=1,
    )
    arrived_down = send_down(packed)
    split_at = lower_face.shape[1] * 24
    got_vectors = arrived_down[:, :split_at].reshape(lower_face.shape)
    got_links = arrived_down[:, split_at:].reshape(link_face.shape)
    unused_two, plus_half = project(got_vectors, direction)
    return (from_above, transport(got_links, plus_half, True))


def complex_mul(first, second):
    return (
        first[0] * second[0] - first[1] * second[1],
        first[0] * second[1] + first[1] * second[0],
    )


def rotate(top_entry, bottom_entry, scale_norm, upper_value, lower_value):
    conj_top = (top_entry[0], -top_entry[1])
    conj_bottom = (bottom_entry[0], -bottom_entry[1])
    part_one = complex_mul(conj_top, upper_value)
    part_two = complex_mul(conj_bottom, lower_value)
    part_three = complex_mul(bottom_entry, upper_value)
    part_four = complex_mul(top_entry, lower_value)
    new_upper = ((part_one[0] + part_two[0]) / scale_norm, (part_one[1] + part_two[1]) / scale_norm)
    new_lower = (
        (part_four[0] - part_three[0]) / scale_norm,
        (part_four[1] - part_three[1]) / scale_norm,
    )
    return (new_upper, new_lower)


def least_squares(hessen, beta):
    columns = len(hessen[0])
    zero_value = jnp.zeros((), jnp.float32)
    matrix = [list(row_list) for row_list in hessen]
    target = [(beta, zero_value)] + [(zero_value, zero_value)] * columns
    rotations = []
    for col_index in range(columns):
        for rot_index in range(col_index):
            top_entry, bottom_entry, scale_norm = rotations[rot_index]
            pair = rotate(
                top_entry,
                bottom_entry,
                scale_norm,
                matrix[rot_index][col_index],
                matrix[rot_index + 1][col_index],
            )
            matrix[rot_index][col_index] = pair[0]
            matrix[rot_index + 1][col_index] = pair[1]
        top_entry = matrix[col_index][col_index]
        bottom_entry = matrix[col_index + 1][col_index]
        scale_norm = jnp.sqrt(
            top_entry[0] * top_entry[0]
            + top_entry[1] * top_entry[1]
            + bottom_entry[0] * bottom_entry[0]
            + bottom_entry[1] * bottom_entry[1]
        )
        rotations.append((top_entry, bottom_entry, scale_norm))
        matrix[col_index][col_index] = (scale_norm, zero_value)
        matrix[col_index + 1][col_index] = (zero_value, zero_value)
        pair = rotate(top_entry, bottom_entry, scale_norm, target[col_index], target[col_index + 1])
        target[col_index] = pair[0]
        target[col_index + 1] = pair[1]
    weights = [None] * columns
    for row_index in reversed(range(columns)):
        remainder = target[row_index]
        for col_index in range(row_index + 1, columns):
            product_term = complex_mul(matrix[row_index][col_index], weights[col_index])
            remainder = (remainder[0] - product_term[0], remainder[1] - product_term[1])
        weights[row_index] = (
            remainder[0] / matrix[row_index][row_index][0],
            remainder[1] / matrix[row_index][row_index][0],
        )
    return weights


def split_two(value):
    high = value.astype(jnp.bfloat16)
    low = (value - high.astype(jnp.float32)).astype(jnp.bfloat16)
    return high, low


def turn(value):
    lane = lax.broadcasted_iota(jnp.int32, value.shape, 1)
    down = pltpu.roll(value, LANES - NV, 1)
    up = pltpu.roll(value, NV, 1)
    return jnp.where(lane < NV, down, jnp.where(lane < 2 * NV, -up, 0.0))


def total(value):
    return jnp.sum(jnp.sum(value, axis=0, keepdims=True), axis=1, keepdims=True)


def gmres_kernel(
    rows_ref, rhs_ref, perm_ref, expand_ref, reduce_ref, pick_ref, op_ref, sol_ref, near_ref, acc_ref
):
    count = rows_ref.shape[0]

    def apply(vector):
        high, low = split_two(vector)
        both = high.astype(jnp.float32) + pltpu.roll(low.astype(jnp.float32), 2 * NV, 1)
        both = both.astype(jnp.bfloat16)
        near_ref[...] = jnp.dot(
            perm_ref[...], both, preferred_element_type=jnp.float32
        ).astype(jnp.bfloat16)

        @pl.loop(0, SLAB // LANES)
        def _(chunk):
            at = pl.multiple_of(chunk * LANES, LANES)
            wide_at = pl.ds(pl.multiple_of(chunk * 2 * LANES, 2 * LANES), 2 * LANES)
            sums = jnp.zeros((count, 2 * LANES), jnp.float32)
            for k in range(9):
                near = near_ref[k * count : (k + 1) * count]
                rows = rows_ref[:, pl.ds(k * SLAB + at, LANES)].astype(jnp.float32)
                wide = jnp.dot(
                    near, expand_ref[:, wide_at], preferred_element_type=jnp.float32
                )
                sums = sums + jnp.concatenate([rows, rows], axis=1) * wide
            acc_ref[:, wide_at] = sums

        high, low = split_two(acc_ref[...])
        return jnp.dot(high, reduce_ref[...], preferred_element_type=jnp.float32) + jnp.dot(
            low, reduce_ref[...], preferred_element_type=jnp.float32
        )

    pick = pick_ref[...]
    for k in range(9):
        op_ref[:, k * SLAB : (k + 1) * SLAB] = jnp.dot(
            pick, rows_ref[:, k * SLAB : (k + 1) * SLAB], preferred_element_type=jnp.float32
        ).astype(jnp.bfloat16)
    right_side = rhs_ref[...]
    zero_value = jnp.zeros((1, 1), jnp.float32)
    beta = jnp.sqrt(total(right_side * right_side) + epsilon)
    basis = [right_side / beta]
    turned = [turn(basis[0])]
    hessen = []
    for row_index in range(ITERS + 1):
        hessen.append([(zero_value, zero_value)] * ITERS)
    for column in range(ITERS):
        work = apply(basis[column])
        for row_index in range(column + 1):
            coef_re = total(basis[row_index] * work)
            coef_im = -total(turned[row_index] * work)
            hessen[row_index][column] = (coef_re, coef_im)
            work = work - coef_re * basis[row_index] + coef_im * turned[row_index]
        norm_now = jnp.sqrt(total(work * work) + epsilon)
        hessen[column + 1][column] = (norm_now, zero_value)
        if column + 1 < ITERS:
            basis.append(work / norm_now)
            turned.append(turn(basis[-1]))
    weights = least_squares(hessen, beta)
    answer = jnp.zeros_like(right_side)
    for column in range(ITERS):
        answer = answer + weights[column][0] * basis[column] - weights[column][1] * turned[column]
    high, low = split_two(answer)
    rest = (answer - high.astype(jnp.float32) - low.astype(jnp.float32)).astype(jnp.bfloat16)
    sol_ref[...] = (
        jnp.dot(pick, high, preferred_element_type=jnp.float32)
        + jnp.dot(pick, low, preferred_element_type=jnp.float32)
        + jnp.dot(pick, rest, preferred_element_type=jnp.float32)
    )


def index_tables(size_z, size_y, size_x):
    count = size_z * size_y * size_x * AT
    where = np.arange(count).reshape(size_z, size_y, size_x, AT)
    perm = np.zeros((9, count, count), np.float32)
    for k, offset in enumerate(neighbor_offsets):
        source = np.roll(where, [-step for step in offset], axis=(0, 1, 2, 3)).reshape(-1)
        perm[k, np.arange(count), source] = 1.0
    lane = np.arange(SLAB)
    comp, row, col = lane // (NV * NV), lane // NV % NV, lane % NV
    expand = np.zeros((LANES, 2, SLAB), np.float32)
    reduce = np.zeros((2, SLAB, LANES), np.float32)
    for half in range(2):
        expand[half * NV + col, half, lane] = 1.0
        expand[(2 + half) * NV + col, half, lane] = 1.0
        out = np.where(comp == half, 0, NV) + row
        reduce[half, lane, out] = np.where((half == 1) & (comp == 1), -1.0, 1.0)
    tiles = SLAB // LANES
    expand = expand.reshape(LANES, 2, tiles, LANES).transpose(0, 2, 1, 3).reshape(LANES, 2 * SLAB)
    reduce = reduce.reshape(2, tiles, LANES, LANES).transpose(1, 0, 2, 3).reshape(2 * SLAB, LANES)
    slots = np.zeros((count // AT, count), np.float32)
    z, y, x, a = np.meshgrid(
        np.arange(size_z), np.arange(size_y), np.arange(size_x), np.arange(AT), indexing="ij"
    )
    slots[((z * size_x + x) * size_y + y).reshape(-1), where.reshape(-1)] = 1.0
    kind = jnp.bfloat16
    return (
        perm.reshape(9 * count, count).astype(kind),
        expand.astype(kind),
        reduce.astype(kind),
        slots.astype(kind),
    )


def coarse_solve(rows, rhs, owner):
    size_z = lax.axis_size("gz")
    size_y = lax.axis_size("gy")
    size_x = lax.axis_size("gx")
    count = rows.shape[0]
    perm, expand, reduce, slots = index_tables(size_z, size_y, size_x)
    mine = (owner.reshape(1, -1) == lax.axis_index(("gz", "gx"))).astype(jnp.bfloat16)
    pick = slots * mine
    padded = jnp.pad(rhs.astype(jnp.float32), ((0, 0), (0, LANES - 2 * NV)))
    return pl.pallas_call(
        gmres_kernel,
        out_shape=(
            jax.ShapeDtypeStruct((count // AT, 9 * SLAB), jnp.bfloat16),
            jax.ShapeDtypeStruct((count // AT, LANES), jnp.float32),
        ),
        in_specs=[pl.BlockSpec(memory_space=pltpu.VMEM)] * 6,
        out_specs=[pl.BlockSpec(memory_space=pltpu.VMEM)] * 2,
        scratch_shapes=[
            pltpu.VMEM((9 * count, LANES), jnp.bfloat16),
            pltpu.VMEM((count, 2 * SLAB), jnp.float32),
        ],
        compiler_params=pltpu.CompilerParams(vmem_limit_bytes=60 << 20),
    )(rows, padded, perm, expand, reduce, pick)


def on_device(vectors, links, site_term, owner, coarse_rhs):
    local_vec = vectors[0, 0, 0]
    local_link = links[0, 0, 0]
    local_site = site_term[0, 0, 0]
    halves = make_halves(local_vec, local_link)
    incoming_x = spinor_faces(
        local_vec,
        local_link,
        0,
        lambda payload: from_behind(payload, "gx", -1),
        lambda payload: from_behind(payload, "gx", 1),
    )
    incoming_y = spinor_faces(
        local_vec,
        local_link,
        1,
        lambda payload: from_behind(payload, "gy", -1),
        lambda payload: from_behind(payload, "gy", 1),
    )
    incoming_z = spinor_faces(
        local_vec,
        local_link,
        2,
        lambda payload: from_behind(payload, "gz", -1),
        lambda payload: from_behind(payload, "gz", 1),
    )
    minus_time, plus_time, back_time = halves[3]
    incoming_t = (
        jnp.roll(select_sites(minus_time, 1, 0), -1, axis=0),
        jnp.roll(select_sites(back_time, 1, 3), 1, axis=0),
    )
    blocks = restrict(
        local_vec, local_link, local_site, halves, [incoming_x, incoming_y, incoming_z, incoming_t]
    )
    rows_flat = blocks.astype(jnp.bfloat16).reshape(blocks.shape[0], -1)
    rhs_flat = coarse_rhs[0, 0, 0].reshape(blocks.shape[0], -1)
    everyone = ("gz", "gy", "gx")
    rows = lax.all_gather(rows_flat, everyone, axis=0, tiled=True)
    rhs = lax.all_gather(rhs_flat, everyone, axis=0, tiled=True)
    operator, answer = coarse_solve(rows, rhs, owner)
    slots = operator.shape[0]
    return (
        operator.reshape(1, slots, 9, 2, NV * NV),
        answer[:, : 2 * NV].reshape(1, slots, 2, NV),
    )


def solution(mesh):
    return jax.shard_map(
        on_device,
        mesh=mesh,
        in_specs=(
            P("gz", "gy", "gx", None, None, None, None, None, None),
            P("gz", "gy", "gx", None, None, None, None, None, None),
            P("gz", "gy", "gx", None, None, None, None, None, None),
            P(),
            P("gz", "gy", "gx", None, None, None),
        ),
        out_specs=(P(("gz", "gx"), None, None, None, None), P(("gz", "gx"), None, None, None)),
        check_vma=False,
    )
```

```python
import jax
import jax.numpy as jnp
import numpy as np
from jax import lax
from jax.experimental import pallas as pl
from jax.experimental.pallas import tpu as pltpu
from jax.sharding import PartitionSpec as P

NV = 24
AT = 4
ITERS = 4
PAIR = 1
LANES = 128
SLAB = 2 * NV * NV


coarse_scale = 1.0 / 256.0
epsilon = 1e-06
site_strides = (64, 16, 4, 1)
neighbor_offsets = (
    (0, 0, 0, 0),
    (0, 0, 1, 0),
    (0, 0, -1, 0),
    (0, 1, 0, 0),
    (0, -1, 0, 0),
    (1, 0, 0, 0),
    (-1, 0, 0, 0),
    (0, 0, 0, 1),
    (0, 0, 0, -1),
)


lower_table = (
    (((1, 3, 1), (0, 3, -1)), ((1, 2, 1), (0, 2, -1))),
    (((0, 3, -1), (1, 3, -1)), ((0, 2, 1), (1, 2, 1))),
    (((1, 2, 1), (0, 2, -1)), ((1, 3, -1), (0, 3, 1))),
    (((0, 2, 1), (1, 2, 1)), ((0, 3, 1), (1, 3, 1))),
)


def from_behind(block, axis, distance):
    devices = range(lax.axis_size(axis))
    route = [((i - distance) % len(devices), i) for i in devices]
    return lax.ppermute(block, axis, route)


def rounded(value):
    return value.astype(jnp.bfloat16).astype(jnp.float32)


def half(vec_ref, direction, spin, colour, sign):
    pair = []
    for part in range(2):
        from_part, from_spin, factor = lower_table[direction][spin][part]
        upper = vec_ref[0, part * 12 + spin * 3 + colour].astype(jnp.float32)
        lower = vec_ref[0, from_part * 12 + from_spin * 3 + colour].astype(jnp.float32)
        pair.append(rounded(upper + (sign * factor) * lower))
    return pair


def link(link_ref, direction, part, row, col):
    at = direction * 18 + part * 9 + row * 3 + col
    return link_ref[0, at : at + 1, :]


def halves_kernel(vec_ref, link_ref, minus_ref, back_ref):
    for mu in range(4):
        for spin in range(2):
            plus = []
            for col in range(3):
                minus = half(vec_ref, mu, spin, col, -1)
                plus.append(half(vec_ref, mu, spin, col, 1))
                for part in range(2):
                    minus_ref[mu, 0, part * 6 + spin * 3 + col] = minus[part].astype(jnp.bfloat16)
            for col in range(3):
                out_re, out_im = 0.0, 0.0
                for row in range(3):
                    u_re = link(link_ref, mu, 0, row, col)
                    u_im = link(link_ref, mu, 1, row, col)
                    p_re, p_im = plus[row]
                    out_re = out_re + u_re * p_re + u_im * p_im
                    out_im = out_im + u_re * p_im - u_im * p_re
                back_ref[mu, 0, spin * 3 + col] = out_re.astype(jnp.bfloat16)
                back_ref[mu, 0, 6 + spin * 3 + col] = out_im.astype(jnp.bfloat16)


def contract(left, right):
    return lax.dot_general(
        jnp.concatenate(left, axis=1),
        jnp.concatenate(right, axis=1),
        (((1,), (1,)), ((), ())),
        preferred_element_type=jnp.float32,
    )


def stacked(pieces):
    return jnp.concatenate(pieces, axis=0).astype(jnp.bfloat16)


def restrict_kernel(vec_ref, link_ref, site_ref, minus_ref, back_ref, *rest):
    near_minus, near_back, out_ref = rest[0:4], rest[4:8], rest[8]
    sites = vec_ref.shape[-1]
    left, right = [], []
    for chirality in range(2):
        for i in range(6):
            out_re, out_im = 0.0, 0.0
            for j in range(6):
                at = chirality * 72 + i * 6 + j
                m_re = site_ref[0, at : at + 1, :]
                m_im = site_ref[0, at + 36 : at + 37, :]
                v_re = vec_ref[0, chirality * 6 + j].astype(jnp.float32)
                v_im = vec_ref[0, 12 + chirality * 6 + j].astype(jnp.float32)
                out_re = out_re + m_re * v_re - m_im * v_im
                out_im = out_im + m_re * v_im + m_im * v_re
            right.append(stacked([out_re, out_im, out_re, out_im]))
            at = chirality * 6 + i
            left.append(
                stacked([vec_ref[0, at].astype(jnp.float32), vec_ref[0, 12 + at].astype(jnp.float32)])
            )
    out_ref[0, 0] = contract(left, right)
    position = lax.broadcasted_iota(jnp.int32, (NV, sites), 1)
    for mu in range(4):
        stride = site_strides[mu]
        coordinate = position // stride % 4
        last = coordinate == 3
        first = coordinate == 0

        def split(pair, edge):
            return stacked(
                [jnp.where(edge, 0.0, part) for part in pair]
                + [jnp.where(edge, part, 0.0) for part in pair]
            )

        def shifted(own, near, edge, own_shift, near_shift):
            return jnp.where(
                edge,
                pltpu.roll(near.astype(jnp.float32), near_shift, 1),
                pltpu.roll(own.astype(jnp.float32), own_shift, 1),
            )

        left, right = [], []
        for spin in range(2):
            field = []
            for col in range(3):
                at = spin * 3 + col
                field.append(
                    [
                        shifted(
                            minus_ref[mu, 0, part * 6 + at],
                            near_minus[mu][0, part * 6 + at],
                            last,
                            sites - stride,
                            3 * stride,
                        )
                        for part in range(2)
                    ]
                )
            for row in range(3):
                out_re, out_im = 0.0, 0.0
                for col in range(3):
                    u_re = link(link_ref, mu, 0, row, col)
                    u_im = link(link_ref, mu, 1, row, col)
                    f_re, f_im = field[col]
                    out_re = out_re + u_re * f_re - u_im * f_im
                    out_im = out_im + u_re * f_im + u_im * f_re
                right.append(split((out_re, out_im), last))
                at = spin * 3 + row
                left.append(
                    stacked([minus_ref[mu, 0, part * 6 + at].astype(jnp.float32) for part in range(2)])
                )
        out_ref[0, 2 * mu + 1] = contract(left, right)
        left, right = [], []
        for spin in range(2):
            for col in range(3):
                at = spin * 3 + col
                pair = [
                    shifted(
                        back_ref[mu, 0, part * 6 + at],
                        near_back[mu][0, part * 6 + at],
                        first,
                        stride,
                        sites - 3 * stride,
                    )
                    for part in range(2)
                ]
                right.append(split(pair, first))
                left.append(stacked(half(vec_ref, mu, spin, col, 1)))
        out_ref[0, 2 * mu + 2] = contract(left, right)


def fine_blocks(vectors, links, site_term):
    sites = vectors.shape[-1]
    vec = jnp.transpose(vectors, (0, 2, 3, 4, 1, 5)).reshape(AT, 24, NV, sites)
    link_f = links.astype(jnp.float32).reshape(AT, 72, sites)
    site_f = site_term.astype(jnp.float32).reshape(AT, 144, sites)
    vec_spec = pl.BlockSpec((1, 24, NV, sites), lambda a: (a, 0, 0, 0))
    link_spec = pl.BlockSpec((1, 72, sites), lambda a: (a, 0, 0))
    site_spec = pl.BlockSpec((1, 144, sites), lambda a: (a, 0, 0))
    half_spec = pl.BlockSpec((4, 1, 12, NV, sites), lambda a: (0, a, 0, 0, 0))
    near_spec = pl.BlockSpec((1, 12, NV, sites), lambda a: (a, 0, 0, 0))
    half_shape = jax.ShapeDtypeStruct((4, AT, 12, NV, sites), jnp.bfloat16)
    params = pltpu.CompilerParams(vmem_limit_bytes=48 << 20)
    minus, back = pl.pallas_call(
        halves_kernel,
        grid=(AT,),
        in_specs=[vec_spec, link_spec],
        out_specs=[half_spec, half_spec],
        out_shape=(half_shape, half_shape),
        compiler_params=params,
    )(vec, link_f)
    axes = ("gx", "gy", "gz")
    near_minus = [from_behind(minus[mu], axes[mu], -1) for mu in range(3)]
    near_back = [from_behind(back[mu], axes[mu], 1) for mu in range(3)]
    near_minus.append(jnp.roll(minus[3], -1, axis=0))
    near_back.append(jnp.roll(back[3], 1, axis=0))
    products = pl.pallas_call(
        restrict_kernel,
        grid=(AT,),
        in_specs=[vec_spec, link_spec, site_spec, half_spec, half_spec] + [near_spec] * 8,
        out_specs=pl.BlockSpec((1, 9, 2 * NV, 4 * NV), lambda a: (a, 0, 0, 0)),
        out_shape=jax.ShapeDtypeStruct((AT, 9, 2 * NV, 4 * NV), jnp.float32),
        compiler_params=params,
    )(vec, link_f, site_f, minus, back, *near_minus, *near_back)
    parts = products.reshape(AT, 9, 2, NV, 2, 2, NV)
    real = parts[:, :, 0, :, :, 0] + parts[:, :, 1, :, :, 1]
    imag = parts[:, :, 0, :, :, 1] - parts[:, :, 1, :, :, 0]
    both = jnp.stack([real, imag], 2)
    inside, outside = both[:, :, :, :, 0], both[:, :, :, :, 1]
    own = (inside[:, :1] - 0.5 * jnp.sum(inside[:, 1:], axis=1, keepdims=True)) * coarse_scale
    return jnp.concatenate([own, outside[:, 1:] * (-0.5 * coarse_scale)], axis=1)


def complex_mul(first, second):
    return (
        first[0] * second[0] - first[1] * second[1],
        first[0] * second[1] + first[1] * second[0],
    )


def rotate(top_entry, bottom_entry, scale_norm, upper_value, lower_value):
    conj_top = (top_entry[0], -top_entry[1])
    conj_bottom = (bottom_entry[0], -bottom_entry[1])
    part_one = complex_mul(conj_top, upper_value)
    part_two = complex_mul(conj_bottom, lower_value)
    part_three = complex_mul(bottom_entry, upper_value)
    part_four = complex_mul(top_entry, lower_value)
    new_upper = ((part_one[0] + part_two[0]) / scale_norm, (part_one[1] + part_two[1]) / scale_norm)
    new_lower = (
        (part_four[0] - part_three[0]) / scale_norm,
        (part_four[1] - part_three[1]) / scale_norm,
    )
    return (new_upper, new_lower)


def least_squares(hessen, beta):
    columns = len(hessen[0])
    zero_value = jnp.zeros((), jnp.float32)
    matrix = [list(row_list) for row_list in hessen]
    target = [(beta, zero_value)] + [(zero_value, zero_value)] * columns
    rotations = []
    for col_index in range(columns):
        for rot_index in range(col_index):
            top_entry, bottom_entry, scale_norm = rotations[rot_index]
            pair = rotate(
                top_entry,
                bottom_entry,
                scale_norm,
                matrix[rot_index][col_index],
                matrix[rot_index + 1][col_index],
            )
            matrix[rot_index][col_index] = pair[0]
            matrix[rot_index + 1][col_index] = pair[1]
        top_entry = matrix[col_index][col_index]
        bottom_entry = matrix[col_index + 1][col_index]
        scale_norm = jnp.sqrt(
            top_entry[0] * top_entry[0]
            + top_entry[1] * top_entry[1]
            + bottom_entry[0] * bottom_entry[0]
            + bottom_entry[1] * bottom_entry[1]
        )
        rotations.append((top_entry, bottom_entry, scale_norm))
        matrix[col_index][col_index] = (scale_norm, zero_value)
        matrix[col_index + 1][col_index] = (zero_value, zero_value)
        pair = rotate(top_entry, bottom_entry, scale_norm, target[col_index], target[col_index + 1])
        target[col_index] = pair[0]
        target[col_index + 1] = pair[1]
    weights = [None] * columns
    for row_index in reversed(range(columns)):
        remainder = target[row_index]
        for col_index in range(row_index + 1, columns):
            product_term = complex_mul(matrix[row_index][col_index], weights[col_index])
            remainder = (remainder[0] - product_term[0], remainder[1] - product_term[1])
        weights[row_index] = (
            remainder[0] / matrix[row_index][row_index][0],
            remainder[1] / matrix[row_index][row_index][0],
        )
    return weights


def split_two(value):
    high = value.astype(jnp.bfloat16)
    low = (value - high.astype(jnp.float32)).astype(jnp.bfloat16)
    return high, low


def turn(value):
    lane = lax.broadcasted_iota(jnp.int32, value.shape, 1)
    down = pltpu.roll(value, LANES - NV, 1)
    up = pltpu.roll(value, NV, 1)
    return jnp.where(lane < NV, down, jnp.where(lane < 2 * NV, -up, 0.0))


def total(value):
    return jnp.sum(jnp.sum(value, axis=0, keepdims=True), axis=1, keepdims=True)


def gmres_kernel(
    rows_ref, rhs_ref, perm_ref, expand_ref, reduce_ref, pick_ref, op_ref, sol_ref, near_ref, acc_ref
):
    count = rows_ref.shape[0]

    def apply(vector):
        high, low = split_two(vector)
        both = high.astype(jnp.float32) + pltpu.roll(low.astype(jnp.float32), 2 * NV, 1)
        both = both.astype(jnp.bfloat16)
        near_ref[...] = jnp.dot(
            perm_ref[...], both, preferred_element_type=jnp.float32
        ).astype(jnp.bfloat16)

        @pl.loop(0, SLAB // LANES)
        def _(chunk):
            at = pl.multiple_of(chunk * LANES, LANES)
            wide_at = pl.ds(pl.multiple_of(chunk * 2 * LANES, 2 * LANES), 2 * LANES)
            sums = jnp.zeros((count, 2 * LANES), jnp.float32)
            for k in range(9):
                near = near_ref[k * count : (k + 1) * count]
                rows = rows_ref[:, pl.ds(k * SLAB + at, LANES)].astype(jnp.float32)
                wide = jnp.dot(
                    near, expand_ref[:, wide_at], preferred_element_type=jnp.float32
                )
                sums = sums + jnp.concatenate([rows, rows], axis=1) * wide
            acc_ref[:, wide_at] = sums

        high, low = split_two(acc_ref[...])
        return jnp.dot(high, reduce_ref[...], preferred_element_type=jnp.float32) + jnp.dot(
            low, reduce_ref[...], preferred_element_type=jnp.float32
        )

    pick = pick_ref[...]
    for k in range(9):
        op_ref[:, k * SLAB : (k + 1) * SLAB] = jnp.dot(
            pick, rows_ref[:, k * SLAB : (k + 1) * SLAB], preferred_element_type=jnp.float32
        ).astype(jnp.bfloat16)
    right_side = rhs_ref[...]
    zero_value = jnp.zeros((1, 1), jnp.float32)
    beta = jnp.sqrt(total(right_side * right_side) + epsilon)
    basis = [right_side / beta]
    turned = [turn(basis[0])]
    hessen = []
    for row_index in range(ITERS + 1):
        hessen.append([(zero_value, zero_value)] * ITERS)
    for column in range(ITERS):
        work = apply(basis[column])
        for row_index in range(column + 1):
            coef_re = total(basis[row_index] * work)
            coef_im = -total(turned[row_index] * work)
            hessen[row_index][column] = (coef_re, coef_im)
            work = work - coef_re * basis[row_index] + coef_im * turned[row_index]
        norm_now = jnp.sqrt(total(work * work) + epsilon)
        hessen[column + 1][column] = (norm_now, zero_value)
        if column + 1 < ITERS:
            basis.append(work / norm_now)
            turned.append(turn(basis[-1]))
    weights = least_squares(hessen, beta)
    answer = jnp.zeros_like(right_side)
    for column in range(ITERS):
        answer = answer + weights[column][0] * basis[column] - weights[column][1] * turned[column]
    high, low = split_two(answer)
    rest = (answer - high.astype(jnp.float32) - low.astype(jnp.float32)).astype(jnp.bfloat16)
    sol_ref[...] = (
        jnp.dot(pick, high, preferred_element_type=jnp.float32)
        + jnp.dot(pick, low, preferred_element_type=jnp.float32)
        + jnp.dot(pick, rest, preferred_element_type=jnp.float32)
    )


def index_tables(size_z, size_y, size_x):
    count = size_z * size_y * size_x * AT
    where = np.arange(count).reshape(size_z, size_y, size_x, AT)
    perm = np.zeros((9, count, count), np.float32)
    for k, offset in enumerate(neighbor_offsets):
        source = np.roll(where, [-step for step in offset], axis=(0, 1, 2, 3)).reshape(-1)
        perm[k, np.arange(count), source] = 1.0
    lane = np.arange(SLAB)
    comp, row, col = lane // (NV * NV), lane // NV % NV, lane % NV
    expand = np.zeros((LANES, 2, SLAB), np.float32)
    reduce = np.zeros((2, SLAB, LANES), np.float32)
    for half in range(2):
        expand[half * NV + col, half, lane] = 1.0
        expand[(2 + half) * NV + col, half, lane] = 1.0
        out = np.where(comp == half, 0, NV) + row
        reduce[half, lane, out] = np.where((half == 1) & (comp == 1), -1.0, 1.0)
    tiles = SLAB // LANES
    expand = expand.reshape(LANES, 2, tiles, LANES).transpose(0, 2, 1, 3).reshape(LANES, 2 * SLAB)
    reduce = reduce.reshape(2, tiles, LANES, LANES).transpose(1, 0, 2, 3).reshape(2 * SLAB, LANES)
    slots = np.zeros((count // AT, count), np.float32)
    z, y, x, a = np.meshgrid(
        np.arange(size_z), np.arange(size_y), np.arange(size_x), np.arange(AT), indexing="ij"
    )
    slots[((z * size_x + x) * size_y + y).reshape(-1), where.reshape(-1)] = 1.0
    kind = jnp.bfloat16
    return (
        perm.reshape(9 * count, count).astype(kind),
        expand.astype(kind),
        reduce.astype(kind),
        slots.astype(kind),
    )


def coarse_solve(rows, rhs, owner):
    size_z = lax.axis_size("gz")
    size_y = lax.axis_size("gy")
    size_x = lax.axis_size("gx")
    count = rows.shape[0]
    perm, expand, reduce, slots = index_tables(size_z, size_y, size_x)
    mine = (owner.reshape(1, -1) == lax.axis_index(("gz", "gx"))).astype(jnp.bfloat16)
    pick = slots * mine
    padded = jnp.pad(rhs.astype(jnp.float32), ((0, 0), (0, LANES - 2 * NV)))
    return pl.pallas_call(
        gmres_kernel,
        out_shape=(
            jax.ShapeDtypeStruct((count // AT, 9 * SLAB), jnp.bfloat16),
            jax.ShapeDtypeStruct((count // AT, LANES), jnp.float32),
        ),
        in_specs=[pl.BlockSpec(memory_space=pltpu.VMEM)] * 6,
        out_specs=[pl.BlockSpec(memory_space=pltpu.VMEM)] * 2,
        scratch_shapes=[
            pltpu.VMEM((9 * count, LANES), jnp.bfloat16),
            pltpu.VMEM((count, 2 * SLAB), jnp.float32),
        ],
        compiler_params=pltpu.CompilerParams(vmem_limit_bytes=60 << 20),
    )(rows, padded, perm, expand, reduce, pick)


def on_device(vectors, links, site_term, owner, coarse_rhs):
    local_vec = vectors[0, 0, 0]
    local_link = links[0, 0, 0]
    local_site = site_term[0, 0, 0]
    blocks = fine_blocks(local_vec, local_link, local_site)
    rows_flat = blocks.astype(jnp.bfloat16).reshape(blocks.shape[0], -1)
    rhs_flat = coarse_rhs[0, 0, 0].reshape(blocks.shape[0], -1)
    everyone = ("gz", "gy", "gx")
    rows = lax.all_gather(rows_flat, everyone, axis=0, tiled=True)
    rhs = lax.all_gather(rhs_flat, everyone, axis=0, tiled=True)
    operator, answer = coarse_solve(rows, rhs, owner)
    slots = operator.shape[0]
    return (
        operator.reshape(1, slots, 9, 2, NV * NV),
        answer[:, : 2 * NV].reshape(1, slots, 2, NV),
    )


def solution(mesh):
    return jax.shard_map(
        on_device,
        mesh=mesh,
        in_specs=(
            P("gz", "gy", "gx", None, None, None, None, None, None),
            P("gz", "gy", "gx", None, None, None, None, None, None),
            P("gz", "gy", "gx", None, None, None, None, None, None),
            P(),
            P("gz", "gy", "gx", None, None, None),
        ),
        out_specs=(P(("gz", "gx"), None, None, None, None), P(("gz", "gx"), None, None, None)),
        check_vma=False,
    )
```
